128 devices in a mesh: sec: 4 (over x), fsdp: 32 (over y, z, core).
Axes of the slice: x: 4, y: 4, z: 4, core: 2. Of those that a mesh axis runs over, the one named last changes fastest.
Arguments:
- tokens: bfloat16 [32768, 2560], P(('sec', 'fsdp')), may hold values from -36 to 36
- pre_gain: float32 [2560], replicated, may hold values from 0.1 to 1.9
- w_z: bfloat16 [2560, 2560], P('fsdp'), may hold values from -0.125 to 0.125
- w_x: bfloat16 [2560, 2560], P('fsdp'), may hold values from -0.125 to 0.125
- w_bc: bfloat16 [2560, 256], P('fsdp'), may hold values from -0.125 to 0.125
- w_dt: bfloat16 [2560, 40], P('fsdp'), may hold values from -0.125 to 0.125
- conv_weight: float32 [4, 2816], replicated, may hold values from -0.5 to 0.5
- conv_bias: float32 [2816], replicated, may hold values from -0.5 to 0.5
- dt_bias: float32 [40], replicated, may hold values from -9 to -2
- a_log: float32 [40], replicated, may hold values from -8 to 0
- d_skip: float32 [40], replicated, may hold values from 0.5 to 1.5
- norm_gain: float32 [2560], replicated, may hold values from 0.1 to 1.9
Outputs:
- mixed: bfloat16 [32768, 2560], P(('sec', 'fsdp'))
The draws below stay inside these ranges and needn't reach their ends.
All inputs are finite; a program needn't handle non-finite values.
Results may differ from the reference program's by a relative error of at most 0.015.
Values may be sent and summed in bfloat16 or wider, within the bound.
A program may use at most 384 MiB of HBM per device.

```python
import math
import jax
import jax.numpy as jnp
from jax import lax

D = 2560
HEADS = 40
HEADDIM = 64
NSTATE = 128
SPAN = 256
CONV_WIDTH = 4
INNER = 2560
SEQ = 32768


def head_mixing(key):
    head_order = jax.random.permutation(jax.random.fold_in(key, 11), HEADS)
    jitter = jax.random.uniform(jax.random.fold_in(key, 13), (HEADS,))
    mixing = (head_order.astype(jnp.float32) + jitter) / HEADS
    fast_rate = 0.04
    slow_rate = 0.5 / SEQ
    head_rate = jnp.exp(math.log(fast_rate) * (1.0 - mixing) + math.log(slow_rate) * mixing)
    target_dt = 0.1 * jnp.sqrt(head_rate / fast_rate)
    return (head_rate, target_dt)


def draw_a_log(key, part):
    head_rate, target_dt = head_mixing(key)
    return jnp.log(head_rate / target_dt).astype(jnp.float32)


def draw_dt_bias(key, part):
    head_rate, target_dt = head_mixing(key)
    return jnp.log(jnp.expm1(target_dt)).astype(jnp.float32)


def draw_tokens(key, part):
    row_scale = jnp.exp(jax.random.uniform(jax.random.fold_in(key, 21), (SEQ, 1), minval=math.log(0.3), maxval=math.log(3.0)))
    col_scale = jnp.exp(jax.random.uniform(jax.random.fold_in(key, 22), (1, D), minval=math.log(0.3), maxval=math.log(3.0)))
    base_part = jnp.clip(jax.random.normal(jax.random.fold_in(key, 23), (SEQ, D)), -4.0, 4.0)
    return (base_part * row_scale * col_scale).astype(jnp.bfloat16)


def block_scale(stream_key, extent, cuts, smallest, largest):
    factor_of = 1.0
    for dim, blocks in cuts:
        steps = jax.random.uniform(jax.random.fold_in(jax.random.fold_in(stream_key, 6), dim), (blocks,), jnp.float32, smallest / len(cuts), largest / len(cuts))
        factor_of = factor_of * jnp.repeat(jnp.exp(steps), extent[dim] // blocks).reshape((-1,) + (1,) * (len(extent) - 1 - dim))
    return factor_of


def bell_draw(own_key, shape, deviation, bound, split=(), kind=jnp.bfloat16):
    level = block_scale(own_key, shape, split, -0.22, 0.18) if split else 1.0
    result = jax.random.normal(own_key, shape, jnp.float32) * deviation * level
    return jnp.minimum(jnp.maximum(result, -bound), bound).astype(kind)


def setup_inputs(seed: int = 0) -> dict:
    streams_of = jax.random.split(jax.random.key(seed), 13)
    return {
        "tokens": draw_tokens(jax.random.fold_in(streams_of[12], 71), 0),
        "pre_gain": jnp.clip(1.0 + 0.18 * jax.random.normal(streams_of[1], (D,), jnp.float32), 0.1, 1.9),
        "w_z": bell_draw(streams_of[2], (D, INNER), D ** -0.5, 0.125, ((0, 32),)),
        "w_x": bell_draw(streams_of[3], (D, INNER), D ** -0.5, 0.125, ((0, 32),)),
        "w_bc": bell_draw(streams_of[4], (D, 2 * NSTATE), D ** -0.5, 0.125, ((0, 32),)),
        "w_dt": bell_draw(streams_of[5], (D, HEADS), D ** -0.5, 0.125, ((0, 32),)),
        "conv_weight": jnp.clip(jax.random.uniform(streams_of[6], (CONV_WIDTH, INNER + 2 * NSTATE), jnp.float32, -0.5, 0.5), -0.5, 0.5),
        "conv_bias": jnp.clip(jax.random.uniform(streams_of[7], (INNER + 2 * NSTATE,), jnp.float32, -0.5, 0.5), -0.5, 0.5),
        "dt_bias": draw_dt_bias(jax.random.fold_in(streams_of[12], 71), 0),
        "a_log": draw_a_log(jax.random.fold_in(streams_of[12], 71), 0),
        "d_skip": jnp.clip(jax.random.uniform(streams_of[10], (HEADS,), jnp.float32, 0.5, 1.5), 0.5, 1.5),
        "norm_gain": jnp.clip(1.0 + 0.18 * jax.random.normal(streams_of[11], (INNER,), jnp.float32), 0.1, 1.9),
    }


EPS = 1e-05

def rms_scale(values, gain_vec):
    mean_square = lax.optimization_barrier(jnp.mean(values * values, axis=-1, keepdims=True))
    return values * lax.rsqrt(mean_square + EPS) * gain_vec

def causal_conv(stacked, kernel, offset_bias):
    kernel_len = kernel.shape[0]
    length = stacked.shape[0] - kernel_len + 1
    summed = offset_bias[None, :]
    for offset in range(kernel_len):
        summed = summed + kernel[offset][None, :] * stacked[offset:offset + length].astype(jnp.float32)
    return jax.nn.silu(summed).astype(jnp.bfloat16)

def block_terms(x_conv, b_conv, c_conv, step_dt, head_rates):
    length = step_dt.shape[1]
    cumulative = jnp.cumsum(step_dt * head_rates, axis=1)
    cum_heads = jnp.swapaxes(cumulative, 1, 2)
    dt_heads = jnp.swapaxes(step_dt, 1, 2)
    inner_dots = jnp.einsum('kqn,ksn->kqs', c_conv.astype(jnp.float32), b_conv.astype(jnp.float32), precision=lax.Precision.HIGHEST)
    causal = lax.broadcasted_iota(jnp.int32, (length, length), 0) >= lax.broadcasted_iota(jnp.int32, (length, length), 1)
    cum_gap = cum_heads[:, :, :, None] - cum_heads[:, :, None, :]
    decays = jnp.where(causal, jnp.exp(-jnp.where(causal, cum_gap, 0.0)), 0.0)
    scores = (decays * dt_heads[:, :, None, :] * inner_dots[:, None, :, :]).astype(jnp.bfloat16)
    y_intra = jnp.einsum('khqs,kshp->kqhp', scores.astype(jnp.float32), x_conv.astype(jnp.float32), precision=lax.Precision.HIGHEST)
    to_end = jnp.exp(-(cumulative[:, -1:, :] - cumulative)) * step_dt
    weighted = (x_conv.astype(jnp.float32) * to_end[..., None]).astype(jnp.bfloat16)
    block_state = jnp.einsum('kshp,ksn->khpn', weighted.astype(jnp.float32), b_conv.astype(jnp.float32), precision=lax.Precision.HIGHEST)
    return (y_intra, block_state, cumulative)

def state_output(c_conv, starts, cumulative):
    reached = jnp.einsum('kqn,khpn->kqhp', c_conv.astype(jnp.float32), starts, precision=lax.Precision.HIGHEST)
    return reached * jnp.exp(-cumulative)[..., None]

def reference(tokens, pre_gain, w_z, w_x, w_bc, w_dt, conv_weight, conv_bias, dt_bias, a_log, d_skip, norm_gain):
    normed = rms_scale(tokens.astype(jnp.float32), pre_gain).astype(jnp.bfloat16)
    grouped = normed.reshape(SEQ // SPAN, SPAN, D)

    def project(row_block):
        return tuple((jnp.dot(row_block, matrix, preferred_element_type=jnp.float32).astype(jnp.bfloat16) for matrix in (w_z, w_x, w_bc, w_dt)))
    z_part, x_part, bc_part, dt_raw = lax.map(project, grouped)
    z_part = z_part.reshape(SEQ, INNER)
    x_part = x_part.reshape(SEQ, INNER)
    bc_part = bc_part.reshape(SEQ, 2 * NSTATE)
    dt_raw = dt_raw.reshape(SEQ, HEADS)
    margin = CONV_WIDTH - 1
    x_conv = causal_conv(jnp.concatenate([jnp.zeros((margin, INNER), jnp.bfloat16), x_part], 0), conv_weight[:, :INNER], conv_bias[:INNER])
    bc_conv = causal_conv(jnp.concatenate([jnp.zeros((margin, 2 * NSTATE), jnp.bfloat16), bc_part], 0), conv_weight[:, INNER:], conv_bias[INNER:])
    step_dt = jax.nn.softplus(dt_raw.astype(jnp.float32) + dt_bias)
    head_rates = jnp.exp(a_log)
    blocks = SEQ // SPAN
    x_blocks = x_conv.reshape(blocks, SPAN, HEADS, HEADDIM)
    b_blocks = bc_conv[:, :NSTATE].reshape(blocks, SPAN, NSTATE)
    c_blocks = bc_conv[:, NSTATE:].reshape(blocks, SPAN, NSTATE)
    dt_blocks = step_dt.reshape(blocks, SPAN, HEADS)

    def span_step(carried, pieces):
        x_one, b_one, c_one, dt_one = pieces
        y_intra, block_state, cumulative = block_terms(x_one[None], b_one[None], c_one[None], dt_one[None], head_rates)
        y_state = state_output(c_one[None], carried[None], cumulative)
        new_state = carried * jnp.exp(-cumulative[0, -1, :])[:, None, None] + block_state[0]
        return (new_state, (y_intra + y_state)[0])
    initial = jnp.zeros((HEADS, HEADDIM, NSTATE), jnp.float32)
    final_state, y_blocks = lax.scan(span_step, initial, (x_blocks, b_blocks, c_blocks, dt_blocks))
    y_total = y_blocks.reshape(SEQ, INNER) + jnp.repeat(d_skip, HEADDIM)[None, :] * x_conv.astype(jnp.float32)
    gated = y_total * jax.nn.silu(z_part.astype(jnp.float32))
    return rms_scale(gated, norm_gain).astype(jnp.bfloat16)
```

```python
import functools

import jax
import jax.numpy as jnp
from jax import lax
from jax.experimental import pallas as pl
from jax.experimental.pallas import tpu as pltpu
from jax.sharding import Mesh
from jax.sharding import PartitionSpec as P

AXES = ("sec", "fy", "fz", "fc")
FSDP = AXES[1:]
MESH = pl.DeviceIdType.MESH
F32, BF16 = jnp.float32, jnp.bfloat16

MODEL = 2560
HALF = 1280
STATE = 128
HEADDIM = 64
HALF_HEADS = 20
TOKENS = 256
CHIP_TOKENS = 512
HALO = 16
CHUNK = 128
CHUNKS = 4
SHARD = 80
FIRST = HALF + 2 * STATE
EPS = 1e-05
LOG2E = 1.4426950408889634
SPLIT = 48

N_GATHER = 2 * 2 * (2 + 2 + 8 + 6)
N_EDGE = 16


def dot(a, b, **kw):
    return jnp.dot(a, b, preferred_element_type=F32, **kw)


def contract(a, b, da, db):
    return lax.dot_general(a, b, (((da,), (db,)), ((), ())), preferred_element_type=F32)


def aligned(i, n):
    return pl.multiple_of(i, n)


class Gather:
    def __init__(self, w, sends, recvs, base, where):
        self.w, self.sends, self.recvs, self.next = w, sends, recvs, base
        self.x, self.y, self.z, self.c = where
        self.all = []
        self.m = {}
        for s in (0, 1):
            for sign in (1, -1):
                self.add("p1", s, sign, 0, 0, 0)
                lo, hi = (0, SPLIT) if sign == 1 else (SPLIT, SHARD)
                self.add("f1", s, sign, 0, -sign, 0, lo, hi)
                for o in (0, -1, 1, 2):
                    self.add("p2", s, sign, 1, o, 0)
            self.add("f2", s, 1, 1, 0, -1)
            self.add("f2", s, -1, 1, 1, 1)
            self.add("f2", s, 1, 1, -1, -1, 0, SHARD - SPLIT)
            self.add("f2", s, -1, 1, -1, 1, SHARD - SPLIT, SHARD)
            self.add("f2", s, 1, 1, 2, -1, 0, SPLIT)
            self.add("f2", s, -1, 1, 2, 1, SPLIT, SHARD)

    def rows(self, s, o1, o2, lo, hi):
        oy, oz = (o1, o2) if s == 0 else (o2, o1)
        yy, zz = (self.y + (oy + 4)) % 4, (self.z + (oz + 4)) % 4
        start = (yy * 4 + zz) * (2 * SHARD) + (s * SHARD + lo)
        return self.w.at[pl.ds(aligned(start, 16), hi - lo), :]

    def add(self, kind, s, sign, which, o1, o2, lo=0, hi=SHARD):
        along_y = (which == 0) == (s == 0)
        if along_y:
            dev = (self.x, (self.y + (sign + 4)) % 4, self.z, self.c)
        else:
            dev = (self.x, self.y, (self.z + (sign + 4)) % 4, self.c)
        k = self.next
        self.next += 1
        src = self.rows(s, o1, o2, lo, hi)
        r1, r2 = (o1 - sign, o2) if which == 0 else (o1, o2 - sign)
        land = self.rows(s, r1, r2, lo, hi)
        out = pltpu.make_async_remote_copy(src, src, self.sends.at[k], self.recvs.at[k], device_id=dev, device_id_type=MESH)
        back = pltpu.make_async_remote_copy(land, land, self.sends.at[k], self.recvs.at[k], device_id=dev, device_id_type=MESH)
        self.m[kind, s, sign, o1] = (out, back)
        self.all.append(out)

    def go(self, *key):
        self.m[key][0].start()

    def got(self, *key):
        self.m[key][1].wait_recv()

    def begin(self):
        for s in (0, 1):
            self.go("p1", s, 1, 0)
            self.go("p1", s, -1, 0)
        for s in (0, 1):
            self.go("p2", s, 1, 0)
            self.go("p2", s, -1, 0)

    def service(self, step):
        for s in (0, 1):
            if step == 0:
                self.got("p1", s, 1, 0)
                self.go("f1", s, 1, -1)
                self.go("p2", s, 1, -1)
                self.go("p2", s, -1, -1)
            elif step == 1:
                self.got("p1", s, -1, 0)
                self.go("f1", s, -1, 1)
                self.go("p2", s, 1, 1)
                self.go("p2", s, -1, 1)
            elif step == 2:
                self.got("p2", s, 1, 0)
                self.go("f2", s, 1, 0)
                self.got("p2", s, -1, 0)
            elif step == 3:
                self.got("f1", s, 1, -1)
                self.got("f1", s, -1, 1)
                self.go("p2", s, 1, 2)
                self.go("p2", s, -1, 2)
            elif step == 4:
                self.got("p2", s, 1, -1)
                self.go("f2", s, 1, -1)
                self.got("p2", s, -1, -1)
                self.go("f2", s, -1, -1)
            elif step == 5:
                self.got("p2", s, 1, 1)
                self.got("p2", s, -1, 1)
                self.go("f2", s, -1, 1)
            elif step == 6:
                self.got("p2", s, 1, 2)
                self.go("f2", s, 1, 2)
                self.got("p2", s, -1, 2)
                self.go("f2", s, -1, 2)
            else:
                for sign, o in ((1, 0), (-1, 1), (1, -1), (-1, -1), (1, 2), (-1, 2)):
                    self.got("f2", s, sign, o)

    def drain(self):
        for out in self.all:
            out.wait_send()


def silu(v):
    return v / (1.0 + jnp.exp(-v))


def kernel(
    tok, par, wx, wz, wbc, wdt, out,
    w1, w2, nt, pre, xc, bc, y, stl, sbuf, rbuf, pbuf, st0, st0f,
    dts, cum, row, e2, tmp, dec, dsk, cs, cr, drow, pfx, xt, xtr, xcs, xcr,
    gs, gr, ss, sss, ssr,
    local_sem, gsend, grecv, esend, erecv, asend, arecv, csend, crecv, bsend, brecv, xsend, xrecv,
):
    x, yy, zz, c = [lax.axis_index(a) for a in AXES]
    plane = yy * 4 + zz
    chip = x * 16 + plane
    sib = (x, yy, zz, 1 - c)

    def chip_dev(s):
        return (s // 16, (s // 4) % 4, s % 4, c)

    def plane_dev(q):
        return (x, q // 4, q % 4, c)

    after, before = (chip + 1) % 64, (chip + 63) % 64

    def remote(src, dst, send, recv, dev):
        return pltpu.make_async_remote_copy(src, dst, send, recv, device_id=dev, device_id_type=MESH)

    barrier = pltpu.get_barrier_semaphore()
    targets = [sib, chip_dev(after), chip_dev(before)]
    targets += [plane_dev((plane + o) % 16) for o in range(1, 16)]
    targets += [((x + o) % 4, yy, zz, c) for o in range(1, 4)]
    for dev in targets:
        pl.semaphore_signal(barrier, inc=1, device_id=dev, device_id_type=MESH)

    mine = pl.ds(aligned((plane * 2 + c) * SHARD, 16), SHARD)
    lane_c = pl.ds(aligned(c * HALF, 128), HALF)
    lane_o = pl.ds(aligned((1 - c) * HALF, 128), HALF)
    bc_c = pl.ds(aligned(c * STATE, 128), STATE)
    bc_o = pl.ds(aligned((1 - c) * STATE, 128), STATE)
    places = ((w1, 0, HALF), (w1, HALF, STATE), (w1, HALF + STATE, STATE), (w2, 0, HALF))
    own = (wx.at[:, lane_c], wbc.at[:, bc_c], wdt, wz.at[:, lane_c])
    others = (wx.at[:, lane_o], wbc.at[:, bc_o], wdt, wz.at[:, lane_o])
    locals_ = [
        pltpu.make_async_copy(src, w.at[mine, pl.ds(at, n)], local_sem.at[k])
        for k, (src, (w, at, n)) in enumerate(zip(own, places))
    ]
    gives = [
        remote(src, w.at[mine, pl.ds(at, n)], esend.at[k], erecv.at[k], sib)
        for k, (src, (w, at, n)) in enumerate(zip(others, places))
    ]
    for copy in locals_:
        copy.start()

    base_rows = aligned(HALO + c * TOKENS, 16)
    gain = par[5:6, 0:MODEL]

    def normalize(r, carry):
        v = tok[pl.ds(aligned(r * 32, 32), 32), :].astype(F32)
        mean = jnp.mean(v * v, axis=-1, keepdims=True)
        nt[pl.ds(aligned(base_rows + r * 32, 16), 32), :] = (v * lax.rsqrt(mean + EPS) * gain).astype(BF16)
        return carry

    pl.semaphore_wait(barrier, len(targets))
    for copy in gives:
        copy.start()
    lax.fori_loop(0, TOKENS // 32, normalize, 0)
    tok_rows = nt.at[pl.ds(base_rows, TOKENS), :]
    swap = remote(tok_rows, tok_rows, esend.at[4], erecv.at[4], sib)
    swap.start()

    where = (x, yy, zz, c)
    g1 = Gather(w1, gsend, grecv, 0, where)
    g2 = Gather(w2, gsend, grecv, N_GATHER // 2, where)
    for k in range(3):
        locals_[k].wait()
        gives[k].wait_recv()
    g1.begin()

    kk = lax.broadcasted_iota(jnp.int32, (2 * STATE, 256), 0) % STATE
    for j in range(HALF // 256):
        ll = (lax.broadcasted_iota(jnp.int32, (2 * STATE, 256), 1) + j * 256) // HEADDIM
        e2[:, j * 256 : (j + 1) * 256] = jnp.where(kk == ll, 1.0, 0.0).astype(BF16)

    def halves(v):
        hi = v.astype(BF16)
        lo = (v - hi.astype(F32)).astype(BF16)
        return jnp.concatenate([hi, lo], axis=1)

    roll_by = (STATE - HALF_HEADS * c) % STATE
    skip = pltpu.roll(jnp.broadcast_to(par[9:10, 0:STATE], (8, STATE)), roll_by, 1)
    dsk[...] = dot(halves(skip), e2[...])

    swap.wait_recv()
    halo_src, halo_dst = nt.at[pl.ds(CHIP_TOKENS, HALO), :], nt.at[pl.ds(0, HALO), :]
    halo = remote(halo_src, halo_dst, esend.at[5], erecv.at[5], chip_dev(after))
    halo.start()
    halo.wait_recv()

    @pl.when(chip == 0)
    def _():
        nt[0:HALO, :] = jnp.zeros((HALO, MODEL), BF16)

    for step in range(7):
        g1.service(step)
    locals_[3].wait()
    gives[3].wait_recv()
    g2.begin()
    g1.service(7)

    def project(j, carry):
        lanes = pl.ds(aligned(j * 256, 256), 256)
        pre[:, lanes] = dot(nt[...], w1[:, lanes])
        return carry

    lax.fori_loop(0, 3, project, 0)
    g2.service(0)
    lax.fori_loop(3, 6, project, 0)
    g2.service(1)

    rate = jnp.exp(par[8:9, 0:STATE]) * LOG2E
    bias = par[7:8, 0:STATE]
    tri = jnp.where(
        lax.broadcasted_iota(jnp.int32, (CHUNK, CHUNK), 0) >= lax.broadcasted_iota(jnp.int32, (CHUNK, CHUNK), 1), 1.0, 0.0
    )

    def steps(i, carry):
        rows = pl.ds(aligned(i * CHUNK, CHUNK), CHUNK)
        raw = pre[pl.ds(aligned(HALO + i * CHUNK, 16), CHUNK), HALF + STATE : FIRST] + bias
        dt = jnp.maximum(raw, 0.0) + jnp.log1p(jnp.exp(-jnp.abs(raw)))
        total = dot(tri, pltpu.roll(dt * rate, roll_by, 1), precision=lax.Precision.HIGHEST)
        dt = pltpu.roll(dt, roll_by, 1)
        dts[rows, :] = dt
        cum[rows, :] = total
        row[i] = (total + jnp.log(dt) * LOG2E).T
        return carry

    lax.fori_loop(0, CHUNKS, steps, 0)
    running = jnp.zeros((1, STATE), F32)
    for i in range(CHUNKS):
        last = cum[i * CHUNK + CHUNK - 1 : (i + 1) * CHUNK, :]
        tmp[i : i + 1, :] = last
        tmp[4 + i : 5 + i, :] = running
        running = running + last
    cs[...] = jnp.broadcast_to(running, (8, STATE))
    cr[plane] = jnp.broadcast_to(running, (8, STATE))
    totals, totals_in = [], []
    for o in range(1, 16):
        q, p = (plane + o) % 16, (plane + (16 - o)) % 16
        totals.append(remote(cs, cr.at[plane], csend.at[o - 1], crecv.at[o - 1], plane_dev(q)))
        totals_in.append(remote(cs, cr.at[p], csend.at[o - 1], crecv.at[o - 1], plane_dev(q)))
    for copy in totals:
        copy.start()
    dec[...] = dot(halves(jnp.exp2(-tmp[...])), e2[...])

    def convolve(at, col):
        taps = [par[k : k + 1, col] for k in range(4)]
        offset = par[4:5, col]
        parts = []
        for r in range(0, CHIP_TOKENS, CHUNK):
            v = offset
            for k in range(4):
                v = v + taps[k] * pre[HALO - 3 + k + r : HALO - 3 + k + r + CHUNK, at]
            parts.append(silu(v).astype(BF16))
        return parts

    bcs = convolve(pl.ds(HALF, STATE), pl.ds(aligned(2 * HALF + c * STATE, 128), STATE))
    for r, part in enumerate(bcs):
        bc[c, r * CHUNK : (r + 1) * CHUNK, :] = part
    swap_bc = remote(bc.at[c], bc.at[c], esend.at[6], erecv.at[6], sib)
    swap_bc.start()

    def conv_x(j, carry):
        at = pl.ds(aligned(j * 128, 128), 128)
        parts = convolve(at, pl.ds(aligned(c * HALF + j * 128, 128), 128))
        for r, part in enumerate(parts):
            xc[r * CHUNK : (r + 1) * CHUNK, at] = part
        return carry

    lax.fori_loop(0, HALF // 128, conv_x, 0)
    g2.service(2)
    swap_bc.wait_recv()

    stl[0] = jnp.zeros((STATE, HALF), F32)

    def states(i, carry):
        rows = pl.ds(aligned(i * CHUNK, CHUNK), CHUNK)
        to_end = halves(jnp.exp2(cum[rows, :] - tmp[pl.ds(i, 1), :]) * dts[rows, :])
        b = bc[0, rows, :]
        for j in range(HALF // 256):
            at = slice(j * 256, (j + 1) * 256)
            weighted = (dot(to_end, e2[:, at]) * xc[rows, at].astype(F32)).astype(BF16)
            stl[i + 1, :, at] = stl[i, :, at] * dec[pl.ds(i, 1), at] + contract(b, weighted, 0, 0)
        return carry

    lax.fori_loop(0, CHUNKS, states, 0)
    for q in range(16):
        sbuf[q] = stl[CHUNKS, q * 8 : (q + 1) * 8, :].astype(BF16)
    rbuf[plane] = sbuf[plane]
    parts_out, parts_in = [], []
    for o in range(1, 16):
        q, p = (plane + o) % 16, (plane + (16 - o)) % 16
        parts_out.append(remote(sbuf.at[q], rbuf.at[plane], asend.at[o - 1], arecv.at[o - 1], plane_dev(q)))
        parts_in.append(remote(sbuf.at[q], rbuf.at[p], asend.at[o - 1], arecv.at[o - 1], plane_dev(q)))
    for copy in parts_out:
        copy.start()
    g2.service(3)

    causal = lax.broadcasted_iota(jnp.int32, (CHUNK, CHUNK), 0) >= lax.broadcasted_iota(jnp.int32, (CHUNK, CHUNK), 1)
    low = jnp.where(lax.broadcasted_iota(jnp.int32, (CHUNK, 128), 1) < HEADDIM, 1.0, 0.0).astype(BF16)
    high = (1.0 - low.astype(F32)).astype(BF16)

    def intra(i, carry):
        rows = pl.ds(aligned(i * CHUNK, CHUNK), CHUNK)
        inner = contract(bc[1, rows, :], bc[0, rows, :], 1, 1)
        for pair in range(HALF_HEADS // 2):
            both = []
            for h in (2 * pair, 2 * pair + 1):
                gap = row[i, h : h + 1, :] - cum[rows, h : h + 1]
                both.append((jnp.exp2(jnp.where(causal, gap, -1e30)) * inner).astype(BF16))
            at = slice(pair * 128, (pair + 1) * 128)
            xp = xc[rows, at]
            spread = jnp.concatenate([xp * low, xp * high], axis=0)
            y[rows, at] = dot(jnp.concatenate(both, axis=1), spread) + dsk[0:1, at] * xp.astype(F32)
        return carry

    lax.fori_loop(0, 2, intra, 0)
    g2.service(4)
    lax.fori_loop(2, CHUNKS, intra, 0)

    for copy in totals_in:
        copy.wait_recv()
    for copy in parts_in:
        copy.wait_recv()
    drow[...] = dot(halves(jnp.exp2(-cr[:, 0, :])), e2[...])

    def prefix(k, state):
        pfx[k] = state
        return state * drow[pl.ds(k, 1), :] + rbuf[k].astype(F32)

    whole = lax.fori_loop(0, 16, prefix, jnp.zeros((8, HALF), F32))
    xt[...] = whole
    plane_total = jnp.zeros((8, STATE), F32)
    for k in range(16):
        plane_total = plane_total + cr[k]
    xcs[...] = plane_total
    sec_out, sec_in = [], []
    for o in range(1, 4):
        q, p = (x + o) % 4, (x + (4 - o)) % 4
        for k, (src, dst) in enumerate(((xt, xtr), (xcs, xcr))):
            n = 2 * (o - 1) + k
            sec_out.append(remote(src, dst.at[x], xsend.at[n], xrecv.at[n], (q, yy, zz, c)))
            sec_in.append(remote(src, dst.at[p], xsend.at[n], xrecv.at[n], (q, yy, zz, c)))
    for copy in sec_out:
        copy.start()
    xtr[x] = whole
    xcr[x] = plane_total
    g2.service(5)
    for copy in sec_in:
        copy.wait_recv()
    enter = jnp.zeros((8, HALF), F32)
    for k in range(3):
        moved = enter * dot(halves(jnp.exp2(-xcr[k])), e2[...]) + xtr[k]
        enter = jnp.where(k < x, moved, enter)

    def begin_states(k, state):
        pbuf[k] = (pfx[k] + state).astype(BF16)
        return state * drow[pl.ds(k, 1), :]

    lax.fori_loop(0, 16, begin_states, enter)
    st0[plane] = pbuf[plane]
    starts_out, starts_in = [], []
    for o in range(1, 16):
        q, p = (plane + o) % 16, (plane + (16 - o)) % 16
        starts_out.append(remote(pbuf.at[q], st0.at[plane], bsend.at[o - 1], brecv.at[o - 1], plane_dev(q)))
        starts_in.append(remote(pbuf.at[q], st0.at[p], bsend.at[o - 1], brecv.at[o - 1], plane_dev(q)))
    for copy in starts_out:
        copy.start()
    g2.service(6)
    for copy in starts_in:
        copy.wait_recv()
    for k in range(16):
        st0f[k * 8 : (k + 1) * 8, :] = st0[k].astype(F32)

    def carried(i, carry):
        rows = pl.ds(aligned(i * CHUNK, CHUNK), CHUNK)
        reach = halves(jnp.exp2(-cum[rows, :]))
        cc = bc[1, rows, :]
        for j in range(HALF // 256):
            at = slice(j * 256, (j + 1) * 256)
            state = (stl[i, :, at] + st0f[:, at] * dec[pl.ds(CHUNKS + i, 1), at]).astype(BF16)
            y[rows, at] = y[rows, at] + dot(cc, state) * dot(reach, e2[:, at])
        return carry

    lax.fori_loop(0, CHUNKS, carried, 0)
    g2.service(7)

    ss[...] = jnp.zeros((CHIP_TOKENS, 128), F32)
    theirs = pl.ds(aligned((1 - c) * TOKENS, TOKENS), TOKENS)
    ours = pl.ds(aligned(c * TOKENS, TOKENS), TOKENS)

    def gate(j, carry):
        at = pl.ds(aligned(j * 256, 256), 256)
        gated = y[:, at] * silu(dot(nt[HALO:, :], w2[:, at]))
        y[:, at] = gated
        square = gated * gated
        ss[...] = ss[...] + square[:, 0:128] + square[:, 128:256]
        gs[:, at] = y[theirs, at].astype(BF16)
        remote(gs.at[:, at], gr.at[:, at], esend.at[8 + j], erecv.at[8 + j], sib).start()
        return carry

    lax.fori_loop(0, HALF // 256, gate, 0)
    sss[...] = ss[theirs, :]
    sums = remote(sss, ssr, esend.at[7], erecv.at[7], sib)
    sums.start()
    sums.wait_recv()
    mean = jnp.sum(ss[ours, :] + ssr[...], axis=-1, keepdims=True) * (1.0 / MODEL)
    scale = lax.rsqrt(mean + EPS)
    for j in range(HALF // 256):
        at = slice(j * 256, (j + 1) * 256)
        spot = pl.ds(aligned(c * HALF + j * 256, 128), 256)
        out[:, spot] = (y[ours, at] * scale * par[6:7, spot]).astype(BF16)
    for j in range(HALF // 256):
        at = slice(j * 256, (j + 1) * 256)
        part = remote(gs.at[:, at], gr.at[:, at], esend.at[8 + j], erecv.at[8 + j], sib)
        part.wait_recv()
        spot = pl.ds(aligned((1 - c) * HALF + j * 256, 128), 256)
        out[:, spot] = (gr[:, at].astype(F32) * scale * par[6:7, spot]).astype(BF16)
        part.wait_send()

    g1.drain()
    g2.drain()
    for copy in gives + [swap, halo, swap_bc, sums] + totals + parts_out + sec_out + starts_out:
        copy.wait_send()


def per_device(
    tokens, pre_gain, w_z, w_x, w_bc, w_dt, conv_weight, conv_bias, dt_bias, a_log, d_skip, norm_gain
):
    width = conv_weight.shape[1]

    def line(v):
        return jnp.pad(v, (0, width - v.shape[0]))[None]

    par = jnp.concatenate(
        [conv_weight, line(conv_bias), line(pre_gain), line(norm_gain), line(dt_bias), line(a_log), line(d_skip)], 0
    )
    wdt = jnp.pad(w_dt, ((0, 0), (0, STATE - w_dt.shape[1])))
    vmem, anywhere = pl.BlockSpec(memory_space=pltpu.VMEM), pl.BlockSpec(memory_space=pl.ANY)
    dma = pltpu.SemaphoreType.DMA
    return pl.pallas_call(
        kernel,
        out_shape=jax.ShapeDtypeStruct((TOKENS, MODEL), BF16),
        in_specs=[vmem, vmem, anywhere, anywhere, anywhere, anywhere],
        out_specs=vmem,
        scratch_shapes=[
            pltpu.VMEM((MODEL, FIRST), BF16),
            pltpu.VMEM((MODEL, HALF), BF16),
            pltpu.VMEM((HALO + CHIP_TOKENS, MODEL), BF16),
            pltpu.VMEM((HALO + CHIP_TOKENS, FIRST), F32),
            pltpu.VMEM((CHIP_TOKENS, HALF), BF16),
            pltpu.VMEM((2, CHIP_TOKENS, STATE), BF16),
            pltpu.VMEM((CHIP_TOKENS, HALF), F32),
            pltpu.VMEM((CHUNKS + 1, STATE, HALF), F32),
            pltpu.VMEM((16, 8, HALF), BF16),
            pltpu.VMEM((16, 8, HALF), BF16),
            pltpu.VMEM((16, 8, HALF), BF16),
            pltpu.VMEM((16, 8, HALF), BF16),
            pltpu.VMEM((STATE, HALF), F32),
            pltpu.VMEM((CHIP_TOKENS, STATE), F32),
            pltpu.VMEM((CHIP_TOKENS, STATE), F32),
            pltpu.VMEM((CHUNKS, STATE, CHUNK), F32),
            pltpu.VMEM((2 * STATE, HALF), BF16),
            pltpu.VMEM((8, STATE), F32),
            pltpu.VMEM((8, HALF), F32),
            pltpu.VMEM((8, HALF), F32),
            pltpu.VMEM((8, STATE), F32),
            pltpu.VMEM((16, 8, STATE), F32),
            pltpu.VMEM((16, HALF), F32),
            pltpu.VMEM((16, 8, HALF), F32),
            pltpu.VMEM((8, HALF), F32),
            pltpu.VMEM((4, 8, HALF), F32),
            pltpu.VMEM((8, STATE), F32),
            pltpu.VMEM((4, 8, STATE), F32),
            pltpu.VMEM((TOKENS, HALF), BF16),
            pltpu.VMEM((TOKENS, HALF), BF16),
            pltpu.VMEM((CHIP_TOKENS, 128), F32),
            pltpu.VMEM((TOKENS, 128), F32),
            pltpu.VMEM((TOKENS, 128), F32),
            dma((4,)),
            dma((N_GATHER,)),
            dma((N_GATHER,)),
            dma((N_EDGE,)),
            dma((N_EDGE,)),
            dma((15,)),
            dma((15,)),
            dma((15,)),
            dma((15,)),
            dma((15,)),
            dma((15,)),
            dma((6,)),
            dma((6,)),
        ],
        compiler_params=pltpu.CompilerParams(
            collective_id=0, has_side_effects=True, vmem_limit_bytes=62 * 1024 * 1024
        ),
    )(tokens, par, w_x, w_z, w_bc, wdt)


def solution(mesh):
    torus = Mesh(mesh.devices.reshape(mesh.shape["sec"], 4, 4, 2), AXES)
    return jax.shard_map(
        per_device,
        mesh=torus,
        in_specs=(
            P(AXES, None), P(), P(FSDP, None), P(FSDP, None), P(FSDP, None), P(FSDP, None),
            P(), P(), P(), P(), P(), P(),
        ),
        out_specs=P(AXES, None),
        check_vma=False,
    )
```

```python
import functools

import jax
import jax.numpy as jnp
from jax import lax
from jax.experimental import pallas as pl
from jax.experimental.pallas import tpu as pltpu
from jax.sharding import Mesh
from jax.sharding import PartitionSpec as P

AXES = ("sec", "fy", "fz", "fc")
FSDP = AXES[1:]
MESH = pl.DeviceIdType.MESH
F32, BF16 = jnp.float32, jnp.bfloat16

MODEL = 2560
HALF = 1280
STATE = 128
HEADDIM = 64
HALF_HEADS = 20
TOKENS = 256
CHIP_TOKENS = 512
HALO = 16
CHUNK = 128
CHUNKS = 4
SHARD = 80
FIRST = HALF + 2 * STATE
EPS = 1e-05
LOG2E = 1.4426950408889634
SPLIT = 48
DIRECT = 96
TILE = 16
WIDTHS = (1024, 512, 768, 512)
NARROW = 2 * STATE
SPOTS = (
    (-1, 0), (1, 0), (0, -1), (0, 1), (2, 0), (-1, -1), (-1, 1), (1, -1), (1, 1), (0, 2), (2, -1), (2, 1), (-1, 2), (1, 2), (2, 2)
)
PER_GATHER = 18 + 15 + 45
N_GATHER = PER_GATHER * len(WIDTHS)
N_EDGE = 20


def dot(a, b, **kw):
    return jnp.dot(a, b, preferred_element_type=F32, **kw)


def contract(a, b, da, db):
    return lax.dot_general(a, b, (((da,), (db,)), ((), ())), preferred_element_type=F32)


def aligned(i, n):
    return pl.multiple_of(i, n)


class Gather:
    def __init__(self, w, sends, recvs, base, where):
        self.w, self.sends, self.recvs, self.next = w, sends, recvs, base
        self.x, self.y, self.z, self.c = where
        self.all = []
        self.m = {}
        for kind in ("d", "q"):
            for sign in (1, -1):
                self.ring(kind + "p1", sign, 0, 0, 0)
                for o in (0, -1, 1, 2):
                    self.ring(kind + "p2", sign, 1, o, 0)
        self.ring("df1", 1, 0, -1, 0, 0, SPLIT)
        self.ring("df1", -1, 0, 1, 0, SPLIT, DIRECT)
        self.ring("df2", 1, 1, 0, -1)
        self.ring("df2", -1, 1, 1, 1)
        for o in (-1, 2):
            self.ring("df2", 1, 1, o, -1, 0, SPLIT)
            self.ring("df2", -1, 1, o, 1, SPLIT, DIRECT)
        self.ring("qf1", 1, 0, -1, 0)
        for sign, o in ((1, 0), (1, 2), (-1, -1), (-1, 1)):
            self.ring("qf2", sign, 1, o, -sign)
        for i, spot in enumerate(SPOTS):
            for sign in (1, -1):
                self.cross("xp", sign, i, spot, 0)
            sign = 1 if i % 2 == 0 else -1
            self.cross("xf", sign, i, spot, 1)

    def place(self, o1, o2):
        c = self.c
        yy = (self.y + (o1 * (1 - c) + o2 * c + 4)) % 4
        zz = (self.z + (o2 * (1 - c) + o1 * c + 4)) % 4
        return yy * 4 + zz

    def tile(self, q):
        return pl.ds(aligned(DIRECT + TILE * ((self.x + (q + 4)) % 4), TILE), TILE)

    def make(self, src, land, dev, key):
        k = self.next
        self.next += 1
        out = pltpu.make_async_remote_copy(src, src, self.sends.at[k], self.recvs.at[k], device_id=dev, device_id_type=MESH)
        back = pltpu.make_async_remote_copy(land, land, self.sends.at[k], self.recvs.at[k], device_id=dev, device_id_type=MESH)
        self.m[key] = (out, back)
        self.all.append(out)

    def ring(self, kind, sign, which, o1, o2, lo=0, hi=DIRECT):
        c = self.c
        along_y = 1 - c if which == 0 else c
        dev = (self.x, (self.y + (sign * along_y + 4)) % 4, (self.z + (sign * (1 - along_y) + 4)) % 4, c)
        rows = pl.ds(lo, hi - lo) if kind[0] == "d" else self.tile(0)
        r1, r2 = (o1 - sign, o2) if which == 0 else (o1, o2 - sign)
        self.make(self.w.at[self.place(o1, o2), rows, :], self.w.at[self.place(r1, r2), rows, :], dev, (kind, sign, o1))

    def cross(self, kind, sign, i, spot, away):
        dev = ((self.x + (sign + 4)) % 4, self.y, self.z, self.c)
        at = self.place(*spot)
        src, land = self.w.at[at, self.tile(-sign * away), :], self.w.at[at, self.tile(-sign * (away + 1)), :]
        self.make(src, land, dev, (kind, sign, i))

    def go(self, kind, sign, o):
        self.m[kind, sign, o][0].start()

    def got(self, kind, sign, o):
        self.m[kind, sign, o][1].wait_recv()

    def both(self, kind, o):
        self.go(kind, 1, o)
        self.go(kind, -1, o)

    def spread(self, *spots):
        for spot in spots:
            self.both("xp", SPOTS.index(spot))

    def qb(self):
        self.both("qp1", 0)
        self.both("qp2", 0)

    def q0(self):
        self.got("qp1", 1, 0)
        self.go("qf1", 1, -1)
        self.both("qp2", -1)
        self.spread((-1, 0))

    def q1(self):
        self.got("qp1", -1, 0)
        self.both("qp2", 1)
        self.spread((1, 0))

    def q2(self):
        self.got("qp2", 1, 0)
        self.go("qf2", 1, 0)
        self.spread((0, -1))
        self.got("qp2", -1, 0)
        self.spread((0, 1))

    def q3(self):
        self.got("qf1", 1, -1)
        self.both("qp2", 2)
        self.spread((2, 0))

    def q4(self):
        self.got("qp2", 1, -1)
        self.spread((-1, -1))
        self.got("qp2", -1, -1)
        self.go("qf2", -1, -1)
        self.spread((-1, 1))
        self.got("qp2", 1, 1)
        self.spread((1, -1))
        self.got("qp2", -1, 1)
        self.go("qf2", -1, 1)
        self.spread((1, 1))

    def q5(self):
        self.got("qf2", 1, 0)
        self.spread((0, 2))
        self.got("qp2", 1, 2)
        self.go("qf2", 1, 2)
        self.spread((2, -1))
        self.got("qp2", -1, 2)
        self.spread((2, 1))

    def q6(self):
        self.got("qf2", -1, -1)
        self.spread((-1, 2))
        self.got("qf2", -1, 1)
        self.spread((1, 2))
        self.got("qf2", 1, 2)
        self.spread((2, 2))

    def x_some(self, lo, hi):
        for i in range(lo, hi):
            for sign in (1, -1):
                self.got("xp", sign, i)
            self.go("xf", 1 if i % 2 == 0 else -1, i)

    def xa(self):
        self.x_some(0, 5)

    def xb(self):
        self.x_some(5, 10)

    def xc(self):
        self.x_some(10, 15)

    def xd(self):
        for i in range(15):
            self.got("xf", 1 if i % 2 == 0 else -1, i)

    def db(self):
        self.both("dp1", 0)

    def dc(self):
        self.both("dp2", 0)

    def d0(self):
        self.got("dp1", 1, 0)
        self.go("df1", 1, -1)
        self.both("dp2", -1)

    def d1(self):
        self.got("dp1", -1, 0)
        self.go("df1", -1, 1)
        self.both("dp2", 1)

    def d2(self):
        self.got("dp2", 1, 0)
        self.go("df2", 1, 0)
        self.got("dp2", -1, 0)

    def d3(self):
        self.got("df1", 1, -1)
        self.got("df1", -1, 1)
        self.both("dp2", 2)

    def d4(self):
        self.got("dp2", 1, -1)
        self.go("df2", 1, -1)
        self.got("dp2", -1, -1)
        self.go("df2", -1, -1)

    def d5(self):
        self.got("dp2", 1, 1)
        self.got("dp2", -1, 1)
        self.go("df2", -1, 1)

    def d6(self):
        self.got("dp2", 1, 2)
        self.go("df2", 1, 2)
        self.got("dp2", -1, 2)
        self.go("df2", -1, 2)

    def d7(self):
        for sign, o in ((1, 0), (-1, 1), (1, -1), (-1, -1), (1, 2), (-1, 2)):
            self.got("df2", sign, o)

    def drain(self):
        for out in self.all:
            out.wait_send()


def silu(v):
    return v / (1.0 + jnp.exp(-v))


def interleave(services, work):
    done = 0
    for i, service in enumerate(services):
        service()
        while done < len(work) and done * len(services) < (i + 1) * len(work):
            work[done]()
            done += 1
    for item in work[done:]:
        item()


def steady(now, then):
    early = [now.q5, now.d0, now.d1, now.xa, now.q6, now.d2, now.d3]
    if then is None:
        return early + [now.xb, now.d4, now.d5, now.d6, now.xc, now.d7, now.xd]
    middle = [then.qb, now.xb, now.d4, now.d5, then.q0, then.q1, then.q2, now.d6, then.db, then.dc]
    return early + middle + [now.xc, then.q3, then.q4, now.d7, now.xd]


def kernel(
    tok_hbm, cw, cb, pg, ng, dtb, alog, dskip, wx, wz, wbc, wdt_t, out,
    w0, w1, w2, w3, tok, wdt, square, small, nt, pre, xc, bc, y, zs, stl, sbuf, rbuf, pbuf, st0, st0f,
    dts, cum, row, e2, tmp, dec, dsk, cs, cr, drow, pfx, xt, xtr, xcs, xcr,
    gs, gr, ss, sss, ssr,
    local_sem, gsend, grecv, esend, erecv, asend, arecv, csend, crecv, bsend, brecv, xsend, xrecv,
):
    x, yy, zz, c = [lax.axis_index(a) for a in AXES]
    plane = yy * 4 + zz
    chip = x * 16 + plane
    sib = (x, yy, zz, 1 - c)

    def chip_dev(s):
        return (s // 16, (s // 4) % 4, s % 4, c)

    def plane_dev(q):
        return (x, q // 4, q % 4, c)

    after, before = (chip + 1) % 64, (chip + 63) % 64

    def remote(src, dst, send, recv, dev):
        return pltpu.make_async_remote_copy(src, dst, send, recv, device_id=dev, device_id_type=MESH)

    barrier = pltpu.get_barrier_semaphore()
    targets = [sib, chip_dev(after), chip_dev(before)]
    targets += [plane_dev((plane + o) % 16) for o in range(1, 16)]
    targets += [((x + o) % 4, yy, zz, c) for o in range(1, 4)]
    for dev in targets:
        pl.semaphore_signal(barrier, inc=1, device_id=dev, device_id_type=MESH)

    def half(core, at, n):
        return pl.ds(aligned(core * HALF + at, 128), n)

    def state_half(core):
        return pl.ds(aligned(core * STATE, 128), STATE)

    def pieces(core):
        return (
            (wbc.at[:, state_half(core)], w0, 0, STATE),
            (wx.at[:, half(core, 0, 768)], w0, NARROW, 768),
            (wx.at[:, half(core, 768, 512)], w1, 0, 512),
            (wz.at[:, half(core, 0, 768)], w2, 0, 768),
            (wz.at[:, half(core, 768, 512)], w3, 0, 512),
            (wdt, w0, STATE, STATE),
        )

    mine = pl.ds(aligned(c * SHARD, 16), SHARD)
    locals_ = [
        pltpu.make_async_copy(src, w.at[plane, mine, pl.ds(at, n)], local_sem.at[k])
        for k, (src, w, at, n) in enumerate(pieces(c))
    ]
    gives = [
        remote(src, w.at[plane, mine, pl.ds(at, n)], esend.at[k], erecv.at[k], sib)
        for k, (src, w, at, n) in enumerate(pieces(1 - c))
    ]
    load = pltpu.make_async_copy(tok_hbm, tok, local_sem.at[6])
    for copy in locals_[:3]:
        copy.start()
    load.start()
    for copy in locals_[3:5]:
        copy.start()
    square[...] = jnp.zeros((STATE, STATE), F32)
    square[0:40, 0:SHARD] = wdt_t[...].astype(F32)
    wdt[...] = square[...].T[0:SHARD, :].astype(BF16)
    locals_[5].start()
    small[...] = jnp.zeros((8, STATE), F32)
    for k, ref in enumerate((dtb, alog, dskip)):
        small[k : k + 1, 0:40] = ref[...]

    pl.semaphore_wait(barrier, len(targets))
    order = (0, 5, 1, 2, 3, 4)
    for k in order:
        gives[k].start()

    def ready(ks):
        for k in ks:
            locals_[k].wait()
            gives[k].wait_recv()

    where = (x, yy, zz, c)
    g = [Gather(w, gsend, grecv, k * PER_GATHER, where) for k, w in enumerate((w0, w1, w2, w3))]
    ready((0, 5, 1))
    g[0].qb()
    g[0].db()
    base_rows = aligned(HALO + c * TOKENS, 16)
    gain = pg[...]

    def normalize(r, carry):
        v = tok[pl.ds(aligned(r * 32, 32), 32), :].astype(F32)
        mean = jnp.mean(v * v, axis=-1, keepdims=True)
        nt[pl.ds(aligned(base_rows + r * 32, 16), 32), :] = (v * lax.rsqrt(mean + EPS) * gain).astype(BF16)
        return carry

    load.wait()
    lax.fori_loop(0, TOKENS // 32, normalize, 0)
    tok_rows = nt.at[pl.ds(base_rows, TOKENS), :]
    swap = remote(tok_rows, tok_rows, esend.at[6], erecv.at[6], sib)
    swap.start()
    g[0].q0()
    g[0].q1()
    g[0].dc()
    g[0].q2()

    kk = lax.broadcasted_iota(jnp.int32, (2 * STATE, 256), 0) % STATE
    for j in range(HALF // 256):
        ll = (lax.broadcasted_iota(jnp.int32, (2 * STATE, 256), 1) + j * 256) // HEADDIM
        e2[:, j * 256 : (j + 1) * 256] = jnp.where(kk == ll, 1.0, 0.0).astype(BF16)

    def halves(v):
        hi = v.astype(BF16)
        lo = (v - hi.astype(F32)).astype(BF16)
        return jnp.concatenate([hi, lo], axis=1)

    g[0].d0()
    g[0].d1()
    swap.wait_recv()
    halo_src, halo_dst = nt.at[pl.ds(CHIP_TOKENS, HALO), :], nt.at[pl.ds(0, HALO), :]
    halo = remote(halo_src, halo_dst, esend.at[7], erecv.at[7], chip_dev(after))
    halo.start()
    for service in (g[0].q3, g[0].q4, g[0].xa, g[0].q5, g[0].d2, g[0].d3, g[0].q6):
        service()
    ready((2,))
    g[1].qb()
    roll_by = (STATE - HALF_HEADS * c) % STATE
    skip = pltpu.roll(jnp.broadcast_to(small[2:3, :], (8, STATE)), roll_by, 1)
    dsk[...] = dot(halves(skip), e2[...])
    for service in (g[0].xb, g[0].d4, g[0].d5, g[1].q0, g[1].q1, g[1].q2, g[0].d6, g[1].db, g[1].dc, g[0].xc):
        service()
    halo.wait_recv()

    @pl.when(chip == 0)
    def _():
        nt[0:HALO, :] = jnp.zeros((HALO, MODEL), BF16)

    for service in (g[1].q3, g[1].q4, g[0].d7, g[0].xd):
        service()

    def project(w, at):
        def body(j, carry):
            lanes = pl.ds(aligned(j * 256, 256), 256)
            pre[:, pl.ds(aligned(at + j * 256, 256), 256)] = dot(nt[...], w[:, :, lanes].reshape(MODEL, 256))
            return carry

        return body

    def loop(lo, hi, body):
        return lambda: lax.fori_loop(lo, hi, body, 0)

    tri = jnp.where(
        lax.broadcasted_iota(jnp.int32, (CHUNK, CHUNK), 0) >= lax.broadcasted_iota(jnp.int32, (CHUNK, CHUNK), 1), 1.0, 0.0
    )

    def steps(i, carry):
        rate = jnp.exp(small[1:2, :]) * LOG2E
        rows = pl.ds(aligned(i * CHUNK, CHUNK), CHUNK)
        raw = pre[pl.ds(aligned(HALO + i * CHUNK, 16), CHUNK), STATE:NARROW] + small[0:1, :]
        dt = jnp.maximum(raw, 0.0) + jnp.log1p(jnp.exp(-jnp.abs(raw)))
        total = dot(tri, pltpu.roll(dt * rate, roll_by, 1), precision=lax.Precision.HIGHEST)
        dt = pltpu.roll(dt, roll_by, 1)
        dts[rows, :] = dt
        cum[rows, :] = total
        row[i] = (total + jnp.log(dt) * LOG2E).T
        return carry

    totals, totals_in = [], []
    for o in range(1, 16):
        q, p = (plane + o) % 16, (plane + (16 - o)) % 16
        totals.append(remote(cs, cr.at[plane], csend.at[o - 1], crecv.at[o - 1], plane_dev(q)))
        totals_in.append(remote(cs, cr.at[p], csend.at[o - 1], crecv.at[o - 1], plane_dev(q)))

    def send_totals():
        running = jnp.zeros((1, STATE), F32)
        for i in range(CHUNKS):
            last = cum[i * CHUNK + CHUNK - 1 : (i + 1) * CHUNK, :]
            tmp[i : i + 1, :] = last
            tmp[4 + i : 5 + i, :] = running
            running = running + last
        cs[...] = jnp.broadcast_to(running, (8, STATE))
        cr[plane] = jnp.broadcast_to(running, (8, STATE))
        for copy in totals:
            copy.start()
        dec[...] = dot(halves(jnp.exp2(-tmp[...])), e2[...])

    def convolve(at, col):
        taps = [cw[k : k + 1, col] for k in range(4)]
        offset = cb[0:1, col]
        parts = []
        for r in range(0, CHIP_TOKENS, CHUNK):
            v = offset
            for k in range(4):
                v = v + taps[k] * pre[HALO - 3 + k + r : HALO - 3 + k + r + CHUNK, at]
            parts.append(silu(v).astype(BF16))
        return parts

    swap_bc = remote(bc.at[c], bc.at[c], esend.at[8], erecv.at[8], sib)

    def conv_bc():
        for r, part in enumerate(convolve(pl.ds(0, STATE), pl.ds(aligned(2 * HALF + c * STATE, 128), STATE))):
            bc[c, r * CHUNK : (r + 1) * CHUNK, :] = part
        swap_bc.start()

    def conv_x(j, carry):
        parts = convolve(pl.ds(aligned(NARROW + j * 128, 128), 128), pl.ds(aligned(c * HALF + j * 128, 128), 128))
        for r, part in enumerate(parts):
            xc[r * CHUNK : (r + 1) * CHUNK, pl.ds(aligned(j * 128, 128), 128)] = part
        return carry

    def states(lo, hi):
        def body(i, carry):
            rows = pl.ds(aligned(i * CHUNK, CHUNK), CHUNK)
            to_end = halves(jnp.exp2(cum[rows, :] - tmp[pl.ds(i, 1), :]) * dts[rows, :])
            b = bc[0, rows, :]
            for j in range(lo, hi):
                at = slice(j * 256, (j + 1) * 256)
                weighted = (dot(to_end, e2[:, at]) * xc[rows, at].astype(F32)).astype(BF16)
                stl[i + 1, :, at] = stl[i, :, at] * dec[pl.ds(i, 1), at] + contract(b, weighted, 0, 0)
            return carry

        return body

    parts_out, parts_in = [], []
    for o in range(1, 16):
        q, p = (plane + o) % 16, (plane + (16 - o)) % 16
        parts_out.append(remote(sbuf.at[q], rbuf.at[plane], asend.at[o - 1], arecv.at[o - 1], plane_dev(q)))
        parts_in.append(remote(sbuf.at[q], rbuf.at[p], asend.at[o - 1], arecv.at[o - 1], plane_dev(q)))

    def send_parts():
        for q in range(16):
            sbuf[q] = stl[CHUNKS, q * 8 : (q + 1) * 8, :].astype(BF16)
        rbuf[plane] = sbuf[plane]
        for copy in parts_out:
            copy.start()

    causal = lax.broadcasted_iota(jnp.int32, (CHUNK, CHUNK), 0) >= lax.broadcasted_iota(jnp.int32, (CHUNK, CHUNK), 1)
    low = jnp.where(lax.broadcasted_iota(jnp.int32, (CHUNK, 128), 1) < HEADDIM, 1.0, 0.0).astype(BF16)
    high = (1.0 - low.astype(F32)).astype(BF16)

    def intra(lo, hi):
        def body(i, carry):
            rows = pl.ds(aligned(i * CHUNK, CHUNK), CHUNK)
            inner = contract(bc[1, rows, :], bc[0, rows, :], 1, 1)
            for pair in range(lo, hi):
                both = []
                for h in (2 * pair, 2 * pair + 1):
                    gap = row[i, h : h + 1, :] - cum[rows, h : h + 1]
                    both.append((jnp.exp2(jnp.where(causal, gap, -1e30)) * inner).astype(BF16))
                at = slice(pair * 128, (pair + 1) * 128)
                xp = xc[rows, at]
                spread = jnp.concatenate([xp * low, xp * high], axis=0)
                y[rows, at] = dot(jnp.concatenate(both, axis=1), spread) + dsk[0:1, at] * xp.astype(F32)
            return carry

        return body

    def zero_states():
        stl[0] = jnp.zeros((STATE, HALF), F32)

    work = [
        loop(0, 1, project(w0, 0)), loop(0, CHUNKS, steps), send_totals, conv_bc,
        loop(1, 2, project(w0, 0)), loop(2, 4, project(w0, 0)), zero_states, loop(0, 6, conv_x), swap_bc.wait_recv,
        loop(0, CHUNKS, states(0, 3)), loop(0, 2, intra(0, 6)), loop(2, CHUNKS, intra(0, 6)),
    ]
    ready((3, 4))
    interleave(steady(g[1], g[2]), work)

    work = [
        loop(0, 2, project(w1, 1024)), loop(6, 10, conv_x), loop(0, CHUNKS, states(3, 5)), send_parts,
        loop(0, 2, intra(6, 10)), loop(2, CHUNKS, intra(6, 10)),
    ]
    flow = steady(g[2], g[3])
    for item in work[:4]:
        item()
        flow.pop(0)()
    interleave(flow, work[4:])

    for copy in totals_in:
        copy.wait_recv()
    for copy in parts_in:
        copy.wait_recv()
    drow[...] = dot(halves(jnp.exp2(-cr[:, 0, :])), e2[...])

    def prefix(k, state):
        pfx[k] = state
        return state * drow[pl.ds(k, 1), :] + rbuf[k].astype(F32)

    whole = lax.fori_loop(0, 16, prefix, jnp.zeros((8, HALF), F32))
    xt[...] = whole
    plane_total = jnp.zeros((8, STATE), F32)
    for k in range(16):
        plane_total = plane_total + cr[k]
    xcs[...] = plane_total
    sec_out, sec_in = [], []
    for o in range(1, 4):
        q, p = (x + o) % 4, (x + (4 - o)) % 4
        for k, (src, dst) in enumerate(((xt, xtr), (xcs, xcr))):
            n = 2 * (o - 1) + k
            sec_out.append(remote(src, dst.at[x], xsend.at[n], xrecv.at[n], (q, yy, zz, c)))
            sec_in.append(remote(src, dst.at[p], xsend.at[n], xrecv.at[n], (q, yy, zz, c)))
    for copy in sec_out:
        copy.start()
    xtr[x] = whole
    xcr[x] = plane_total

    def zdot(w, at):
        def body(j, carry):
            lanes = pl.ds(aligned(j * 256, 256), 256)
            v = dot(nt[HALO:, :], w[:, :, lanes].reshape(MODEL, 256))
            zs[:, pl.ds(aligned(at + j * 256, 256), 256)] = v
            return carry

        return body

    flow = steady(g[3], None)
    interleave(flow[:6], [loop(0, 2, zdot(w2, 0))])
    for copy in sec_in:
        copy.wait_recv()
    enter = jnp.zeros((8, HALF), F32)
    for k in range(3):
        moved = enter * dot(halves(jnp.exp2(-xcr[k])), e2[...]) + xtr[k]
        enter = jnp.where(k < x, moved, enter)

    def begin_states(k, state):
        pbuf[k] = (pfx[k] + state).astype(BF16)
        return state * drow[pl.ds(k, 1), :]

    lax.fori_loop(0, 16, begin_states, enter)
    st0[plane] = pbuf[plane]
    starts_out, starts_in = [], []
    for o in range(1, 16):
        q, p = (plane + o) % 16, (plane + (16 - o)) % 16
        starts_out.append(remote(pbuf.at[q], st0.at[plane], bsend.at[o - 1], brecv.at[o - 1], plane_dev(q)))
        starts_in.append(remote(pbuf.at[q], st0.at[p], bsend.at[o - 1], brecv.at[o - 1], plane_dev(q)))
    for copy in starts_out:
        copy.start()
    interleave(flow[6:], [loop(2, 3, zdot(w2, 0))])
    lax.fori_loop(0, 2, zdot(w3, 768), 0)
    for copy in starts_in:
        copy.wait_recv()
    for k in range(16):
        st0f[k * 8 : (k + 1) * 8, :] = st0[k].astype(F32)

    def finish(i, r, theirs):
        rows = pl.ds(aligned(i * CHUNK, CHUNK), CHUNK)
        reach = halves(jnp.exp2(-cum[rows, :]))
        cc = bc[1, rows, :]
        total = jnp.zeros((CHUNK, 128), F32)
        for j in range(HALF // 256):
            at = slice(j * 256, (j + 1) * 256)
            state = (stl[i, :, at] + st0f[:, at] * dec[pl.ds(CHUNKS + i, 1), at]).astype(BF16)
            gated = (y[rows, at] + dot(cc, state) * dot(reach, e2[:, at])) * silu(zs[rows, at])
            if theirs:
                gs[r * CHUNK : (r + 1) * CHUNK, at] = gated.astype(BF16)
            else:
                y[rows, at] = gated
            squares = gated * gated
            total = total + squares[:, 0:128] + squares[:, 128:256]
        if theirs:
            sss[r * CHUNK : (r + 1) * CHUNK, :] = total
        else:
            ss[r * CHUNK : (r + 1) * CHUNK, :] = total

    swaps = []
    for r in range(2):
        finish((1 - c) * 2 + r, r, True)
        for k, (a, b) in enumerate(((gs, gr), (sss, ssr))):
            part = pl.ds(r * CHUNK, CHUNK)
            n = 10 + 2 * r + k
            swaps.append(remote(a.at[part, :], b.at[part, :], esend.at[n], erecv.at[n], sib))
            swaps[-1].start()
    for r in range(2):
        finish(c * 2 + r, r, False)
    for copy in swaps:
        copy.wait_recv()
    mean = jnp.sum(ss[...] + ssr[...], axis=-1, keepdims=True) * (1.0 / MODEL)
    scale = lax.rsqrt(mean + EPS)
    ours = pl.ds(aligned(c * TOKENS, TOKENS), TOKENS)
    for j in range(HALF // 256):
        at = slice(j * 256, (j + 1) * 256)
        spot = half(c, j * 256, 256)
        out[:, spot] = (y[ours, at] * scale * ng[0:1, spot]).astype(BF16)
        spot = half(1 - c, j * 256, 256)
        out[:, spot] = (gr[:, at].astype(F32) * scale * ng[0:1, spot]).astype(BF16)

    for gather in g:
        gather.drain()
    for copy in gives + [swap, halo, swap_bc] + totals + parts_out + sec_out + starts_out + swaps:
        copy.wait_send()


def per_device(
    tokens, pre_gain, w_z, w_x, w_bc, w_dt, conv_weight, conv_bias, dt_bias, a_log, d_skip, norm_gain
):
    lines = [v.reshape(1, -1) for v in (conv_bias, pre_gain, norm_gain, dt_bias, a_log, d_skip)]
    vmem, anywhere = pl.BlockSpec(memory_space=pltpu.VMEM), pl.BlockSpec(memory_space=pl.ANY)
    dma = pltpu.SemaphoreType.DMA
    return pl.pallas_call(
        kernel,
        out_shape=jax.ShapeDtypeStruct((TOKENS, MODEL), BF16),
        in_specs=[anywhere] + [vmem] * 7 + [anywhere] * 3 + [vmem],
        out_specs=vmem,
        scratch_shapes=[pltpu.VMEM((16, 2 * SHARD, n), BF16) for n in WIDTHS]
        + [
            pltpu.VMEM((TOKENS, MODEL), BF16),
            pltpu.VMEM((SHARD, STATE), BF16),
            pltpu.VMEM((STATE, STATE), F32),
            pltpu.VMEM((8, STATE), F32),
            pltpu.VMEM((HALO + CHIP_TOKENS, MODEL), BF16),
            pltpu.VMEM((HALO + CHIP_TOKENS, FIRST), F32),
            pltpu.VMEM((CHIP_TOKENS, HALF), BF16),
            pltpu.VMEM((2, CHIP_TOKENS, STATE), BF16),
            pltpu.VMEM((CHIP_TOKENS, HALF), F32),
            pltpu.VMEM((CHIP_TOKENS, HALF), F32),
            pltpu.VMEM((CHUNKS + 1, STATE, HALF), F32),
            pltpu.VMEM((16, 8, HALF), BF16),
            pltpu.VMEM((16, 8, HALF), BF16),
            pltpu.VMEM((16, 8, HALF), BF16),
            pltpu.VMEM((16, 8, HALF), BF16),
            pltpu.VMEM((STATE, HALF), F32),
            pltpu.VMEM((CHIP_TOKENS, STATE), F32),
            pltpu.VMEM((CHIP_TOKENS, STATE), F32),
            pltpu.VMEM((CHUNKS, STATE, CHUNK), F32),
            pltpu.VMEM((2 * STATE, HALF), BF16),
            pltpu.VMEM((8, STATE), F32),
            pltpu.VMEM((8, HALF), F32),
            pltpu.VMEM((8, HALF), F32),
            pltpu.VMEM((8, STATE), F32),
            pltpu.VMEM((16, 8, STATE), F32),
            pltpu.VMEM((16, HALF), F32),
            pltpu.VMEM((16, 8, HALF), F32),
            pltpu.VMEM((8, HALF), F32),
            pltpu.VMEM((4, 8, HALF), F32),
            pltpu.VMEM((8, STATE), F32),
            pltpu.VMEM((4, 8, STATE), F32),
            pltpu.VMEM((TOKENS, HALF), BF16),
            pltpu.VMEM((TOKENS, HALF), BF16),
            pltpu.VMEM((TOKENS, 128), F32),
            pltpu.VMEM((TOKENS, 128), F32),
            pltpu.VMEM((TOKENS, 128), F32),
            dma((7,)),
            dma((N_GATHER,)),
            dma((N_GATHER,)),
            dma((N_EDGE,)),
            dma((N_EDGE,)),
            dma((15,)),
            dma((15,)),
            dma((15,)),
            dma((15,)),
            dma((15,)),
            dma((15,)),
            dma((6,)),
            dma((6,)),
        ],
        compiler_params=pltpu.CompilerParams(
            collective_id=0, has_side_effects=True, vmem_limit_bytes=62 * 1024 * 1024
        ),
    )(tokens, conv_weight, *lines, w_x, w_z, w_bc, w_dt.T)


def solution(mesh):
    torus = Mesh(mesh.devices.reshape(mesh.shape["sec"], 4, 4, 2), AXES)
    return jax.shard_map(
        per_device,
        mesh=torus,
        in_specs=(
            P(AXES, None), P(), P(FSDP, None), P(FSDP, None), P(FSDP, None), P(FSDP, None),
            P(), P(), P(), P(), P(), P(),
        ),
        out_specs=P(AXES, None),
        check_vma=False,
    )
```

```python
import functools

import jax
import jax.numpy as jnp
from jax import lax
from jax.experimental import pallas as pl
from jax.experimental.pallas import tpu as pltpu
from jax.sharding import Mesh
from jax.sharding import PartitionSpec as P

AXES = ("sec", "fy", "fz", "fc")
FSDP = AXES[1:]
MESH = pl.DeviceIdType.MESH
F32, BF16 = jnp.float32, jnp.bfloat16

MODEL = 2560
HALF = 1280
STATE = 128
HEADDIM = 64
HALF_HEADS = 20
TOKENS = 256
CHIP_TOKENS = 512
HALO = 16
CHUNK = 128
CHUNKS = 4
SHARD = 80
FIRST = HALF + 2 * STATE
EPS = 1e-05
LOG2E = 1.4426950408889634
WIDTHS = (1024, 512, 768, 512)
TILES = (16, 16, 16, 32)
NARROW = 2 * STATE
SPOTS = (
    (-1, 0), (1, 0), (0, -1), (0, 1), (2, 0), (-1, -1), (-1, 1), (1, -1), (1, 1), (0, 2), (2, -1), (2, 1), (-1, 2), (1, 2), (2, 2)
)
GROUPS = {
    "d0": 1, "d1": 1, "d2": 2, "d3": 1, "d4": 2, "d5": 2, "d6": 2, "d7": 4,
    "q0": 1, "q1": 1, "q2": 2, "q3": 1, "q4": 4, "q5": 3, "q6": 3, "xa": 10, "xb": 10, "xc": 10, "xd": 15
}
NAMES = list(GROUPS)
N_EDGE = 14


def dot(a, b, **kw):
    return jnp.dot(a, b, preferred_element_type=F32, **kw)


def contract(a, b, da, db):
    return lax.dot_general(a, b, (((da,), (db,)), ((), ())), preferred_element_type=F32)


def aligned(i, n):
    return pl.multiple_of(i, n)


class Gather:
    def __init__(self, w, sends, recvs, number, where):
        self.w, self.sent, self.recvs, self.number = w, sends.at[number], recvs, number
        self.x, self.y, self.z, self.c = where
        self.eager = number == 0
        self.rows = TILES[number]
        direct = self.direct = 2 * SHARD - 4 * self.rows
        split = direct // 2
        self.m = {}
        for kind in ("d", "q"):
            for sign in (1, -1):
                self.ring(kind + "p1", sign, 0, 0, 0, "0" if sign == 1 else "1")
                for o, group in zip((0, -1, 1, 2), "2456" if kind == "d" else "2445"):
                    self.ring(kind + "p2", sign, 1, o, 0, group)
        self.ring("df1", 1, 0, -1, 0, "3", 0, split)
        self.ring("df1", -1, 0, 1, 0, "3", split, direct)
        self.ring("df2", 1, 1, 0, -1, "7")
        self.ring("df2", -1, 1, 1, 1, "7")
        for o in (-1, 2):
            self.ring("df2", 1, 1, o, -1, "7", 0, split)
            self.ring("df2", -1, 1, o, 1, "7", split, direct)
        self.turn = 1 if number % 2 == 0 else -1
        self.ring("qf1", self.turn, 0, -self.turn, 0, "3")
        for sign, o, group in ((1, 0, "5"), (1, 2, "6"), (-1, -1, "6"), (-1, 1, "6")):
            self.ring("qf2", sign, 1, o, -sign, group)
        for i, spot in enumerate(SPOTS):
            for sign in (1, -1):
                self.cross("xp", sign, i, spot, 0, "x" + "abc"[i // 5])
            sign = 1 if i % 2 == 0 else -1
            self.cross("xf", sign, i, spot, 1, "xd")

    def place(self, o1, o2):
        c = self.c
        yy = (self.y + (o1 * (1 - c) + o2 * c + 4)) % 4
        zz = (self.z + (o2 * (1 - c) + o1 * c + 4)) % 4
        return yy * 4 + zz

    def tile(self, q):
        return pl.ds(aligned(self.direct + self.rows * ((self.x + (q + 4)) % 4), 16), self.rows)

    def arrival(self, group):
        return self.recvs.at[self.number * len(NAMES) + NAMES.index(group)]

    def ring(self, kind, sign, which, o1, o2, group, lo=0, hi=None):
        c = self.c
        along_y = 1 - c if which == 0 else c
        dev = (self.x, (self.y + (sign * along_y + 4)) % 4, (self.z + (sign * (1 - along_y) + 4)) % 4, c)
        rows = pl.ds(lo, (hi or self.direct) - lo) if kind[0] == "d" else self.tile(0)
        src = self.w.at[self.place(o1, o2), rows, :]
        self.m[kind, sign, o1] = (src, dev, self.arrival(kind[0] + group))

    def cross(self, kind, sign, i, spot, away, group):
        dev = ((self.x + (sign + 4)) % 4, self.y, self.z, self.c)
        src = self.w.at[self.place(*spot), self.tile(-sign * away), :]
        self.m[kind, sign, i] = (src, dev, self.arrival(group))

    def go(self, kind, sign, o):
        src, dev, arrival = self.m[kind, sign, o]
        pltpu.make_async_remote_copy(src, src, self.sent, arrival, device_id=dev, device_id_type=MESH).start()

    def got(self, group):
        chips, rows = GROUPS[group], self.direct if group[0] == "d" else self.rows
        land = self.w.at[pl.ds(0, chips), pl.ds(0, rows), :]
        me = (self.x, self.y, self.z, 1 - self.c)
        pltpu.make_async_remote_copy(land, land, self.sent, self.arrival(group), device_id=me, device_id_type=MESH).wait_recv()

    def both(self, kind, o):
        self.go(kind, 1, o)
        self.go(kind, -1, o)

    def spread(self, *spots):
        if self.eager:
            for spot in spots:
                self.both("xp", SPOTS.index(spot))

    def sp(self):
        for i in range(len(SPOTS)):
            self.both("xp", i)

    def qb(self):
        self.both("qp1", 0)
        self.both("qp2", 0)

    def q0(self):
        self.got("q0")
        if self.turn == 1:
            self.go("qf1", 1, -1)
        self.both("qp2", -1)
        self.spread((-1, 0))

    def q1(self):
        self.got("q1")
        if self.turn == -1:
            self.go("qf1", -1, 1)
        self.both("qp2", 1)
        self.spread((1, 0))

    def q2(self):
        self.got("q2")
        self.go("qf2", 1, 0)
        self.spread((0, -1), (0, 1))

    def q3(self):
        self.got("q3")
        self.both("qp2", 2)
        self.spread((2, 0))

    def q4(self):
        self.got("q4")
        self.go("qf2", -1, -1)
        self.go("qf2", -1, 1)
        self.spread((-1, -1), (-1, 1), (1, -1), (1, 1))

    def q5(self):
        self.got("q5")
        self.go("qf2", 1, 2)
        self.spread((0, 2), (2, -1), (2, 1))

    def q6(self):
        self.got("q6")
        self.spread((-1, 2), (1, 2), (2, 2))

    def x_some(self, group, lo, hi):
        self.got(group)
        for i in range(lo, hi):
            self.go("xf", 1 if i % 2 == 0 else -1, i)

    def xa(self):
        self.x_some("xa", 0, 5)

    def xb(self):
        self.x_some("xb", 5, 10)

    def xc(self):
        self.x_some("xc", 10, 15)

    def xd(self):
        self.got("xd")

    def db(self):
        self.both("dp1", 0)

    def dc(self):
        self.both("dp2", 0)

    def d0(self):
        self.got("d0")
        self.go("df1", 1, -1)
        self.both("dp2", -1)

    def d1(self):
        self.got("d1")
        self.go("df1", -1, 1)
        self.both("dp2", 1)

    def d2(self):
        self.got("d2")
        self.go("df2", 1, 0)

    def d3(self):
        self.got("d3")
        self.both("dp2", 2)

    def d4(self):
        self.got("d4")
        self.both("df2", -1)

    def d5(self):
        self.got("d5")
        self.go("df2", -1, 1)

    def d6(self):
        self.got("d6")
        self.both("df2", 2)

    def d7(self):
        self.got("d7")

    def drain(self):
        every = self.w.at[pl.ds(0, 15), :, :]
        me = (self.x, self.y, self.z, 1 - self.c)
        pltpu.make_async_remote_copy(every, every, self.sent, self.arrival("d0"), device_id=me, device_id_type=MESH).wait_send()


def silu(v):
    return v / (1.0 + jnp.exp(-v))


def interleave(services, work):
    done = 0
    for i, service in enumerate(services):
        service()
        while done < len(work) and done * len(services) < (i + 1) * len(work):
            work[done]()
            done += 1
    for item in work[done:]:
        item()


def steady(now, then, later):
    flow = [then.db, then.dc, then.xa, now.d4, now.d5, then.xb, now.d6]
    if later is not None:
        flow.append(later.sp)
    return flow + [then.d0, then.d1, then.xc, then.d2, then.d3, now.d7, now.xd]


def kernel(
    tok_hbm, cw, cb, pg, ng, dtb, alog, dskip, wx, wz, wbc, wdt_t, out,
    w0, w1, w2, w3, tok, wdt, square, small, nt, pre, xc, bc, y, zs, stl, sbuf, rbuf, pbuf, st0, st0f,
    dts, cum, row, e2, tmp, dec, dsk, cs, cr, drow, pfx, xt, xtr, xcs, xcr,
    gs, gr, ss, sss, ssr,
    local_sem, gsend, grecv, esend, erecv, asend, arecv, xsend, xrecv,
):
    x, yy, zz, c = [lax.axis_index(a) for a in AXES]
    plane = yy * 4 + zz
    chip = x * 16 + plane
    sib = (x, yy, zz, 1 - c)

    def chip_dev(s):
        return (s // 16, (s // 4) % 4, s % 4, c)

    def plane_dev(q):
        return (x, q // 4, q % 4, c)

    after, before = (chip + 1) % 64, (chip + 63) % 64

    def remote(src, dst, send, recv, dev):
        return pltpu.make_async_remote_copy(src, dst, send, recv, device_id=dev, device_id_type=MESH)

    barrier = pltpu.get_barrier_semaphore()
    targets = [sib, chip_dev(after), chip_dev(before)]
    targets += [plane_dev((plane + o) % 16) for o in range(1, 16)]
    targets += [((x + o) % 4, yy, zz, c) for o in range(1, 4)]
    for dev in targets:
        pl.semaphore_signal(barrier, inc=1, device_id=dev, device_id_type=MESH)

    def half(core, at, n):
        return pl.ds(aligned(core * HALF + at, 128), n)

    def state_half(core):
        return pl.ds(aligned(core * STATE, 128), STATE)

    def pieces(core):
        return (
            (wbc.at[:, state_half(core)], w0, 0, STATE),
            (wx.at[:, half(core, 0, 768)], w0, NARROW, 768),
            (wx.at[:, half(core, 768, 512)], w1, 0, 512),
            (wz.at[:, half(core, 0, 768)], w2, 0, 768),
            (wz.at[:, half(core, 768, 512)], w3, 0, 512),
            (wdt, w0, STATE, STATE),
        )

    mine = pl.ds(aligned(c * SHARD, 16), SHARD)
    locals_ = [
        pltpu.make_async_copy(src, w.at[plane, mine, pl.ds(at, n)], local_sem.at[k])
        for k, (src, w, at, n) in enumerate(pieces(c))
    ]
    gives = [
        remote(src, w.at[plane, mine, pl.ds(at, n)], esend.at[k], erecv.at[k], sib)
        for k, (src, w, at, n) in enumerate(pieces(1 - c))
    ]
    load = pltpu.make_async_copy(tok_hbm, tok, local_sem.at[6])
    for copy in locals_[:3]:
        copy.start()
    load.start()
    for copy in locals_[3:5]:
        copy.start()
    square[...] = jnp.zeros((STATE, STATE), F32)
    square[0:40, 0:SHARD] = wdt_t[...].astype(F32)
    wdt[...] = square[...].T[0:SHARD, :].astype(BF16)
    locals_[5].start()
    small[...] = jnp.zeros((8, STATE), F32)
    for k, ref in enumerate((dtb, alog, dskip)):
        small[k : k + 1, 0:40] = ref[...]

    pl.semaphore_wait(barrier, len(targets))
    order = (0, 5, 1, 2, 3, 4)
    for k in order:
        gives[k].start()

    def ready(ks):
        for k in ks:
            locals_[k].wait()
            gives[k].wait_recv()

    where = (x, yy, zz, c)
    g = [Gather(w, gsend, grecv, k, where) for k, w in enumerate((w0, w1, w2, w3))]
    ready((0, 5, 1))
    g[0].qb()
    ready((2,))
    g[1].qb()
    ready((3, 4))
    g[2].qb()
    g[3].qb()
    base_rows = aligned(HALO + c * TOKENS, 16)

    def normalize(r, carry):
        v = tok[pl.ds(aligned(r * 32, 32), 32), :].astype(F32)
        mean = jnp.mean(v * v, axis=-1, keepdims=True)
        scale = lax.rsqrt(mean + EPS)
        for j in range(MODEL // 128):
            at = slice(j * 128, (j + 1) * 128)
            nt[pl.ds(aligned(base_rows + r * 32, 16), 32), at] = (v[:, at] * scale * pg[j : j + 1, :]).astype(BF16)
        return carry

    load.wait()
    lax.fori_loop(0, TOKENS // 32, normalize, 0)
    tok_rows = nt.at[pl.ds(base_rows, TOKENS), :]
    swap = remote(tok_rows, tok_rows, esend.at[6], erecv.at[6], sib)
    swap.start()

    def tiles(step):
        for gather in g:
            getattr(gather, step)()

    tiles("q0")
    tiles("q1")
    tiles("q2")

    kk = lax.broadcasted_iota(jnp.int32, (2 * STATE, 256), 0) % STATE
    for j in range(HALF // 256):
        ll = (lax.broadcasted_iota(jnp.int32, (2 * STATE, 256), 1) + j * 256) // HEADDIM
        e2[:, j * 256 : (j + 1) * 256] = jnp.where(kk == ll, 1.0, 0.0).astype(BF16)

    def halves(v):
        hi = v.astype(BF16)
        lo = (v - hi.astype(F32)).astype(BF16)
        return jnp.concatenate([hi, lo], axis=1)

    tiles("q3")
    g[0].db()
    tiles("q4")
    g[0].dc()
    swap.wait_recv()
    halo_src, halo_dst = nt.at[pl.ds(CHIP_TOKENS, HALO), :], nt.at[pl.ds(0, HALO), :]
    halo = remote(halo_src, halo_dst, esend.at[7], erecv.at[7], chip_dev(after))
    halo.start()
    tiles("q5")
    g[0].xa()
    g[0].d0()
    g[0].d1()
    tiles("q6")
    g[0].xb()
    g[1].sp()
    g[0].d2()
    g[0].d3()
    g[0].xc()
    roll_by = (STATE - HALF_HEADS * c) % STATE
    skip = pltpu.roll(jnp.broadcast_to(small[2:3, :], (8, STATE)), roll_by, 1)
    dsk[...] = dot(halves(skip), e2[...])
    flow = steady(g[0], g[1], g[2])
    for service in flow[:-2]:
        service()
    halo.wait_recv()

    @pl.when(chip == 0)
    def _():
        nt[0:HALO, :] = jnp.zeros((HALO, MODEL), BF16)

    for service in flow[-2:]:
        service()

    def project(w, at):
        def body(j, carry):
            lanes = pl.ds(aligned(j * 256, 256), 256)
            pre[:, pl.ds(aligned(at + j * 256, 256), 256)] = dot(nt[...], w[:, :, lanes].reshape(MODEL, 256))
            return carry

        return body

    def loop(lo, hi, body, unroll=False):
        return lambda: lax.fori_loop(lo, hi, body, 0, unroll=unroll)

    tri = jnp.where(
        lax.broadcasted_iota(jnp.int32, (CHUNK, CHUNK), 0) >= lax.broadcasted_iota(jnp.int32, (CHUNK, CHUNK), 1), 1.0, 0.0
    )

    def steps(i, carry):
        rate = jnp.exp(small[1:2, :]) * LOG2E
        rows = pl.ds(aligned(i * CHUNK, CHUNK), CHUNK)
        raw = pre[pl.ds(aligned(HALO + i * CHUNK, 16), CHUNK), STATE:NARROW] + small[0:1, :]
        dt = jnp.maximum(raw, 0.0) + jnp.log1p(jnp.exp(-jnp.abs(raw)))
        total = dot(tri, pltpu.roll(dt * rate, roll_by, 1), precision=lax.Precision.HIGHEST)
        dt = pltpu.roll(dt, roll_by, 1)
        dts[rows, :] = dt
        cum[rows, :] = total
        row[i] = (total + jnp.log(dt) * LOG2E).T
        return carry

    def exchange(src_of, dst, send, recv):
        out = []
        for o in range(1, 16):
            q = (plane + o) % 16
            out.append(remote(src_of(q), dst.at[plane], send, recv, plane_dev(q)))
        everything = remote(dst.at[pl.ds(0, 15)], dst.at[pl.ds(0, 15)], send, recv, sib)
        return out, everything

    totals, totals_all = exchange(lambda q: cs, cr, asend.at[0], arecv.at[0])

    def send_totals():
        running = jnp.zeros((1, STATE), F32)
        for i in range(CHUNKS):
            last = cum[i * CHUNK + CHUNK - 1 : (i + 1) * CHUNK, :]
            tmp[i : i + 1, :] = last
            tmp[4 + i : 5 + i, :] = running
            running = running + last
        cs[...] = jnp.broadcast_to(running, (8, STATE))
        cr[plane] = jnp.broadcast_to(running, (8, STATE))
        for copy in totals:
            copy.start()
        dec[...] = dot(halves(jnp.exp2(-tmp[...])), e2[...])

    def convolve(at, block):
        taps = [cw[k : k + 1, pl.ds(aligned(block * 128, 128), 128)] for k in range(4)]
        offset = cb[pl.ds(block, 1), :]
        parts = []
        for r in range(0, CHIP_TOKENS, CHUNK):
            v = offset
            for k in range(4):
                v = v + taps[k] * pre[HALO - 3 + k + r : HALO - 3 + k + r + CHUNK, at]
            parts.append(silu(v).astype(BF16))
        return parts

    swap_bc = remote(bc.at[c], bc.at[c], esend.at[8], erecv.at[8], sib)

    def conv_bc():
        for r, part in enumerate(convolve(pl.ds(0, STATE), 2 * HALF // 128 + c)):
            bc[c, r * CHUNK : (r + 1) * CHUNK, :] = part
        swap_bc.start()

    def conv_x(j, carry):
        parts = convolve(pl.ds(aligned(NARROW + j * 128, 128), 128), c * (HALF // 128) + j)
        for r, part in enumerate(parts):
            xc[r * CHUNK : (r + 1) * CHUNK, pl.ds(aligned(j * 128, 128), 128)] = part
        return carry

    def states(lo, hi):
        def body(i, carry):
            rows = pl.ds(aligned(i * CHUNK, CHUNK), CHUNK)
            to_end = halves(jnp.exp2(cum[rows, :] - tmp[pl.ds(i, 1), :]) * dts[rows, :])
            b = bc[0, rows, :]
            for j in range(lo, hi):
                at = slice(j * 256, (j + 1) * 256)
                weighted = (dot(to_end, e2[:, at]) * xc[rows, at].astype(F32)).astype(BF16)
                stl[i + 1, :, at] = stl[i, :, at] * dec[pl.ds(i, 1), at] + contract(b, weighted, 0, 0)
            return carry

        return body

    parts_out, parts_all = exchange(lambda q: sbuf.at[q], rbuf, asend.at[1], arecv.at[1])

    def send_parts():
        for q in range(16):
            sbuf[q] = stl[CHUNKS, q * 8 : (q + 1) * 8, :].astype(BF16)
        rbuf[plane] = sbuf[plane]
        for copy in parts_out:
            copy.start()

    causal = lax.broadcasted_iota(jnp.int32, (CHUNK, CHUNK), 0) >= lax.broadcasted_iota(jnp.int32, (CHUNK, CHUNK), 1)
    low = jnp.where(lax.broadcasted_iota(jnp.int32, (CHUNK, 128), 1) < HEADDIM, 1.0, 0.0).astype(BF16)
    high = (1.0 - low.astype(F32)).astype(BF16)

    def intra(lo, hi):
        def body(i, carry):
            rows = pl.ds(aligned(i * CHUNK, CHUNK), CHUNK)
            inner = contract(bc[1, rows, :], bc[0, rows, :], 1, 1)
            for pair in range(lo, hi):
                both = []
                for h in (2 * pair, 2 * pair + 1):
                    gap = row[i, h : h + 1, :] - cum[rows, h : h + 1]
                    both.append((jnp.exp2(jnp.where(causal, gap, -1e30)) * inner).astype(BF16))
                at = slice(pair * 128, (pair + 1) * 128)
                xp = xc[rows, at]
                spread = jnp.concatenate([xp * low, xp * high], axis=0)
                y[rows, at] = dot(jnp.concatenate(both, axis=1), spread) + dsk[0:1, at] * xp.astype(F32)
            return carry

        return body

    def zero_states():
        stl[0] = jnp.zeros((STATE, HALF), F32)

    work = [
        loop(0, 2, project(w0, 0)), loop(0, CHUNKS, steps, True), send_totals, conv_bc,
        loop(2, 4, project(w0, 0)), zero_states, loop(0, 6, conv_x), swap_bc.wait_recv,
        loop(0, CHUNKS, states(0, 3), True),
    ]
    interleave(steady(g[1], g[2], g[3]), work)

    def run(*items):
        for item in items:
            item()

    run(loop(0, 2, project(w1, 1024)), g[2].d4, g[2].d5, loop(6, 10, conv_x))
    run(g[2].d6, g[3].db, g[3].dc, loop(0, CHUNKS, states(3, 5), True), send_parts, g[3].xa)
    run(loop(0, 2, intra(0, 10)), g[3].xb, g[3].d0, g[3].d1, loop(2, CHUNKS, intra(0, 10)), g[3].d2, g[3].xc, g[3].d3, g[3].d4)
    totals_all.wait_recv()
    parts_all.wait_recv()
    drow[...] = dot(halves(jnp.exp2(-cr[:, 0, :])), e2[...])

    def prefix(k, state):
        pfx[k] = state
        return state * drow[pl.ds(k, 1), :] + rbuf[k].astype(F32)

    whole = lax.fori_loop(0, 16, prefix, jnp.zeros((8, HALF), F32))
    xt[...] = whole
    plane_total = jnp.zeros((8, STATE), F32)
    for k in range(16):
        plane_total = plane_total + cr[k]
    xcs[...] = plane_total
    sec_out, sec_in = [], []
    for o in range(1, 4):
        q, p = (x + o) % 4, (x + (4 - o)) % 4
        for k, (src, dst) in enumerate(((xt, xtr), (xcs, xcr))):
            n = 2 * (o - 1) + k
            sec_out.append(remote(src, dst.at[x], xsend.at[n], xrecv.at[n], (q, yy, zz, c)))
            sec_in.append(remote(src, dst.at[p], xsend.at[n], xrecv.at[n], (q, yy, zz, c)))
    for copy in sec_out:
        copy.start()
    xtr[x] = whole
    xcr[x] = plane_total

    def zdot(w, at):
        def body(j, carry):
            lanes = pl.ds(aligned(j * 256, 256), 256)
            v = dot(nt[HALO:, :], w[:, :, lanes].reshape(MODEL, 256))
            zs[:, pl.ds(aligned(at + j * 256, 256), 256)] = v
            return carry

        return body

    run(g[3].d5, g[3].d6, g[2].d7, g[2].xd, loop(0, 2, zdot(w2, 0)))
    for copy in sec_in:
        copy.wait_recv()
    enter = jnp.zeros((8, HALF), F32)
    for k in range(3):
        moved = enter * dot(halves(jnp.exp2(-xcr[k])), e2[...]) + xtr[k]
        enter = jnp.where(k < x, moved, enter)

    def begin_states(k, state):
        pbuf[k] = (pfx[k] + state).astype(BF16)
        return state * drow[pl.ds(k, 1), :]

    lax.fori_loop(0, 16, begin_states, enter)
    st0[plane] = pbuf[plane]
    starts_out, starts_all = exchange(lambda q: pbuf.at[q], st0, asend.at[2], arecv.at[2])
    for copy in starts_out:
        copy.start()
    run(loop(2, 3, zdot(w2, 0)), g[3].d7, g[3].xd)
    lax.fori_loop(0, 2, zdot(w3, 768), 0)
    starts_all.wait_recv()
    for k in range(16):
        st0f[k * 8 : (k + 1) * 8, :] = st0[k].astype(F32)

    def finish(i, r, theirs):
        rows = pl.ds(aligned(i * CHUNK, CHUNK), CHUNK)
        reach = halves(jnp.exp2(-cum[rows, :]))
        cc = bc[1, rows, :]
        total = jnp.zeros((CHUNK, 128), F32)
        for j in range(HALF // 256):
            at = slice(j * 256, (j + 1) * 256)
            state = (stl[i, :, at] + st0f[:, at] * dec[pl.ds(CHUNKS + i, 1), at]).astype(BF16)
            gated = (y[rows, at] + dot(cc, state) * dot(reach, e2[:, at])) * silu(zs[rows, at])
            if theirs:
                gs[r * CHUNK : (r + 1) * CHUNK, at] = gated.astype(BF16)
            else:
                y[rows, at] = gated
            squares = gated * gated
            total = total + squares[:, 0:128] + squares[:, 128:256]
        if theirs:
            sss[r * CHUNK : (r + 1) * CHUNK, :] = total
        else:
            ss[r * CHUNK : (r + 1) * CHUNK, :] = total

    swaps = []
    for r in range(2):
        finish((1 - c) * 2 + r, r, True)
        for k, (a, b) in enumerate(((gs, gr), (sss, ssr))):
            part = pl.ds(r * CHUNK, CHUNK)
            n = 10 + 2 * r + k
            swaps.append(remote(a.at[part, :], b.at[part, :], esend.at[n], erecv.at[n], sib))
            swaps[-1].start()
    for r in range(2):
        finish(c * 2 + r, r, False)
    for copy in swaps:
        copy.wait_recv()
    mean = jnp.sum(ss[...] + ssr[...], axis=-1, keepdims=True) * (1.0 / MODEL)
    scale = lax.rsqrt(mean + EPS)
    ours = pl.ds(aligned(c * TOKENS, TOKENS), TOKENS)
    for j in range(HALF // 128):
        at = slice(j * 128, (j + 1) * 128)
        gain = ng[pl.ds(c * (HALF // 128) + j, 1), :]
        out[:, half(c, j * 128, 128)] = (y[ours, at] * scale * gain).astype(BF16)
        gain = ng[pl.ds((1 - c) * (HALF // 128) + j, 1), :]
        out[:, half(1 - c, j * 128, 128)] = (gr[:, at].astype(F32) * scale * gain).astype(BF16)

    for gather in g:
        gather.drain()
    for copy in gives + [swap, halo, swap_bc, totals_all, parts_all, starts_all] + sec_out + swaps:
        copy.wait_send()


def per_device(
    tokens, pre_gain, w_z, w_x, w_bc, w_dt, conv_weight, conv_bias, dt_bias, a_log, d_skip, norm_gain
):
    lines = [v.reshape(-1, 128) for v in (conv_bias, pre_gain, norm_gain)]
    lines += [v.reshape(1, -1) for v in (dt_bias, a_log, d_skip)]
    vmem, anywhere = pl.BlockSpec(memory_space=pltpu.VMEM), pl.BlockSpec(memory_space=pl.ANY)
    dma = pltpu.SemaphoreType.DMA
    return pl.pallas_call(
        kernel,
        out_shape=pltpu.VMEM((TOKENS, MODEL), BF16),
        in_specs=[anywhere] + [vmem] * 7 + [anywhere] * 3 + [vmem],
        out_specs=vmem,
        scratch_shapes=[pltpu.VMEM((16, 2 * SHARD, n), BF16) for n in WIDTHS]
        + [
            pltpu.VMEM((TOKENS, MODEL), BF16),
            pltpu.VMEM((SHARD, STATE), BF16),
            pltpu.VMEM((STATE, STATE), F32),
            pltpu.VMEM((8, STATE), F32),
            pltpu.VMEM((HALO + CHIP_TOKENS, MODEL), BF16),
            pltpu.VMEM((HALO + CHIP_TOKENS, FIRST), F32),
            pltpu.VMEM((CHIP_TOKENS, HALF), BF16),
            pltpu.VMEM((2, CHIP_TOKENS, STATE), BF16),
            pltpu.VMEM((CHIP_TOKENS, HALF), F32),
            pltpu.VMEM((CHIP_TOKENS, HALF), F32),
            pltpu.VMEM((CHUNKS + 1, STATE, HALF), F32),
            pltpu.VMEM((16, 8, HALF), BF16),
            pltpu.VMEM((16, 8, HALF), BF16),
            pltpu.VMEM((16, 8, HALF), BF16),
            pltpu.VMEM((16, 8, HALF), BF16),
            pltpu.VMEM((STATE, HALF), F32),
            pltpu.VMEM((CHIP_TOKENS, STATE), F32),
            pltpu.VMEM((CHIP_TOKENS, STATE), F32),
            pltpu.VMEM((CHUNKS, STATE, CHUNK), F32),
            pltpu.VMEM((2 * STATE, HALF), BF16),
            pltpu.VMEM((8, STATE), F32),
            pltpu.VMEM((8, HALF), F32),
            pltpu.VMEM((8, HALF), F32),
            pltpu.VMEM((8, STATE), F32),
            pltpu.VMEM((16, 8, STATE), F32),
            pltpu.VMEM((16, HALF), F32),
            pltpu.VMEM((16, 8, HALF), F32),
            pltpu.VMEM((8, HALF), F32),
            pltpu.VMEM((4, 8, HALF), F32),
            pltpu.VMEM((8, STATE), F32),
            pltpu.VMEM((4, 8, STATE), F32),
            pltpu.VMEM((TOKENS, HALF), BF16),
            pltpu.VMEM((TOKENS, HALF), BF16),
            pltpu.VMEM((TOKENS, 128), F32),
            pltpu.VMEM((TOKENS, 128), F32),
            pltpu.VMEM((TOKENS, 128), F32),
            dma((7,)),
            dma((4,)),
            dma((4 * len(NAMES),)),
            dma((N_EDGE,)),
            dma((N_EDGE,)),
            dma((3,)),
            dma((3,)),
            dma((6,)),
            dma((6,)),
        ],
        compiler_params=pltpu.CompilerParams(
            collective_id=0, has_side_effects=True, vmem_limit_bytes=62 * 1024 * 1024
        ),
    )(tokens, conv_weight, *lines, w_x, w_z, w_bc, w_dt.T)


def solution(mesh):
    torus = Mesh(mesh.devices.reshape(mesh.shape["sec"], 4, 4, 2), AXES)
    return jax.shard_map(
        per_device,
        mesh=torus,
        in_specs=(
            P(AXES, None), P(), P(FSDP, None), P(FSDP, None), P(FSDP, None), P(FSDP, None),
            P(), P(), P(), P(), P(), P(),
        ),
        out_specs=P(AXES, None),
        check_vma=False,
    )
```
